512 devices in a mesh: ka: 32 (over x, z), ba: 16 (over y, core).
Axes of the slice: x: 4, y: 8, z: 8, core: 2. Of those that a mesh axis runs over, the one named last changes fastest.
Arguments:
- density: float32 [2, 8192, 4096], P(None, 'ka', 'ba'), may hold values from -6 to 6
- h_bands: float32 [2, 8192, 4096], P(None, ('ka', 'ba')), may hold values from -0.75 to 0.75
- coupling: bfloat16 [64, 4, 128, 128], P('ka'), may hold values from -0.03125 to 0.03125
- donors: int32 [64, 4], P('ka'), may hold values from 0 to 63, as said below
- counts: int32 [64], P('ka'), may hold values from 2 to 4, as said below
Outputs:
- evolved: float32 [2, 8192, 4096], P(None, 'ka', 'ba')
The draws below stay inside these ranges and needn't reach their ends.
Inputs may be any that keep to these rules, and one draw needn't show every extreme that they name: donors[t] holds 4 different tiles, each within 2 tiles of t in the cyclic order of the 64 tiles; donors[t, 0] = t. `counts`: some tile uses all 4 slots.
All inputs are finite; a program needn't handle non-finite values.
Results may differ from the reference program's by a relative error of at most 0.0013.
Values may be sent and summed in bfloat16 or wider, within the bound.
A program may use at most 64 MiB of HBM per device.

```python
import jax
import jax.numpy as jnp
from jax import lax

NB = 64
TILE = 128
ND = 4
REACH = 2
PAIRS = 4096
TILES = 64
MOM = 8192


def draw_donors(key, part):
    subkeys = jax.random.split(key, TILES)
    others = 2 * REACH

    def single_row(subkey):
        shuffled = jax.random.permutation(subkey, others).astype(jnp.int32)
        nearby = jnp.where(shuffled < REACH, shuffled - REACH, shuffled - REACH + 1)
        return jnp.concatenate([jnp.zeros((1,), jnp.int32), nearby[:ND - 1]])
    offsets = jax.vmap(single_row)(subkeys)
    return ((jnp.arange(TILES, dtype=jnp.int32)[:, None] + offsets) % TILES).astype(jnp.int32)


def draw_counts(key, part):
    key_values = jax.random.fold_in(key, 11)
    key_place = jax.random.fold_in(key, 23)
    values = jax.random.randint(key_values, (TILES,), 2, ND + 1).astype(jnp.int32)
    where_full = jax.random.randint(key_place, (), 0, TILES)
    return values.at[where_full].set(ND).astype(jnp.int32)


def steps_of(own_key, extent, cuts, low, top_value):
    gain, own = 1.0, jax.random.fold_in(own_key, 6)
    for dim, shards_of in cuts:
        draws = jnp.exp(jax.random.uniform(jax.random.fold_in(own, dim), (shards_of,), jnp.float32, low / len(cuts), top_value / len(cuts)))
        gain = gain * jnp.repeat(draws, extent[dim] // shards_of).reshape([-1 if axis == dim else 1 for axis in range(len(extent))])
    return gain


def centred(stream_key, extent, scale, most, shards=(), kind=jnp.bfloat16):
    entries = jax.random.normal(stream_key, extent, jnp.float32) * scale
    if len(shards) > 0:
        entries = steps_of(stream_key, extent, shards, -0.22, 0.18) * entries
    return jnp.clip(entries, min=-most, max=most).astype(kind)


def setup_inputs(seed: int = 0) -> dict:
    keys = jax.random.split(jax.random.key(seed), 6)
    return {
        "density": centred(keys[0], (2, MOM, PAIRS), 1.0, 6.0, ((1, 32), (2, 16)), jnp.float32),
        "h_bands": centred(keys[1], (2, MOM, PAIRS), 0.125, 0.75, ((1, 512),), jnp.float32),
        "coupling": centred(keys[2], (TILES, ND, TILE, TILE), (ND * TILE * NB) ** -0.5, 0.03125, ((0, 32),)),
        "donors": draw_donors(jax.random.fold_in(keys[5], 71), 0),
        "counts": draw_counts(jax.random.fold_in(keys[5], 71), 0),
    }


step_size = 0.25


def commute(hamilton, state):
    count = state.shape[1]
    h_real = hamilton[0].reshape(count, NB, NB)
    h_imag = hamilton[1].reshape(count, NB, NB)
    s_real = state[0].reshape(count, NB, NB)
    s_imag = state[1].reshape(count, NB, NB)

    def product(left, right):
        return jnp.einsum("mab,mbc->mac", left, right, precision=lax.Precision.HIGHEST)

    c_real = product(h_real, s_real) - product(h_imag, s_imag) - product(s_real, h_real) + product(s_imag, h_imag)
    c_imag = product(h_real, s_imag) + product(h_imag, s_real) - product(s_real, h_imag) - product(s_imag, h_real)
    return jnp.stack([c_imag, -c_real]).reshape(2, count, NB * NB)


def reference(density, h_bands, coupling, donors, counts):
    active = (jnp.arange(ND, dtype=jnp.int32)[None, :] < counts[:, None]).astype(jnp.bfloat16)
    masked = coupling * active[:, :, None, None]

    def self_energy(state):
        rounded = state.astype(jnp.bfloat16).reshape(2, TILES, TILE, PAIRS)

        def single(pair):
            weights, indices = pair
            picked = rounded[:, indices].astype(jnp.float32)
            return jnp.einsum("skq,csqp->ckp", weights.astype(jnp.float32), picked, precision=lax.Precision.HIGHEST)

        result = lax.map(single, (masked, donors))
        return -jnp.transpose(result, (1, 0, 2, 3)).reshape(2, MOM, PAIRS)

    def tendency(state):
        return commute(h_bands + self_energy(state), state)

    rate_one = tendency(density)
    middle = density + 0.5 * step_size * rate_one
    rate_two = tendency(middle)
    return density + step_size * rate_two
```

```python
import functools

import jax
import jax.numpy as jnp
from jax import lax
from jax.experimental import pallas as pl
from jax.experimental.pallas import tpu as pltpu
from jax.sharding import PartitionSpec as P

NB = 64
TILE = 128
ND = 4
REACH = 2
TILES = 64
GROUP = 16
ROWS = 64
MESH = pl.DeviceIdType.MESH
F32, BF16, I16 = jnp.float32, jnp.bfloat16, jnp.int16
TOP = 32760.0

step_size = 0.25


def low_half(shape):
    return lax.broadcasted_iota(jnp.int32, shape, len(shape) - 1) < NB


def merge(real, imag):
    low = low_half(real.shape)
    first = jnp.where(low, real, pltpu.roll(imag, NB, 1))
    second = jnp.where(low, pltpu.roll(real, NB, 1), imag)
    return first, second


def split(first, second):
    low = low_half(first.shape)
    real = jnp.where(low, first, pltpu.roll(second, NB, 1))
    imag = jnp.where(low, pltpu.roll(first, NB, 1), second)
    return real, imag


def encode(values):
    top = jnp.max(jnp.abs(values), axis=0, keepdims=True)
    top = jnp.maximum(top, 1e-30)
    codes = jnp.round(values * (TOP / top)).astype(jnp.int32).astype(I16)
    return codes, top * (1.0 / TOP)


def decode(codes, scale):
    return codes.astype(jnp.int32).astype(F32) * scale


def halves(values):
    high = values.astype(BF16)
    return high, (values - high.astype(F32)).astype(BF16)


def rate(hamilton, state):
    sign = jnp.where(low_half(state.shape), 1.0, -1.0).astype(F32)
    turned_s = pltpu.roll(state, NB, 1) * sign
    turned_h = pltpu.roll(hamilton, NB, 1) * sign
    right_high, right_low = halves(
        jnp.concatenate([turned_s, state, turned_h, hamilton], axis=0)
    )
    left_high, left_low = halves(jnp.concatenate([hamilton, -state], axis=1))
    left = jnp.concatenate([left_high, left_low], axis=0)
    right = jnp.concatenate([right_high, right_low], axis=1)
    out = jnp.dot(left, right, preferred_element_type=F32)
    return out[:NB, :TILE] + (out[:NB, TILE:] + out[NB:, :TILE])


def kernel(
    dens_hbm, h_hbm, coup_hbm, donors, counts, out_hbm,
    dens, hraw, coup, low0, halo0, mix, hband, state, ham, rate_two, sigma,
    enc_s, enc_r, scale_s, scale_r, mid_s, mid_r, halo1, out_v,
    load_sem, out_sem, enc_ss, enc_rs, scale_ss, scale_rs,
    mid_ss, mid_rs, halo0_ss, halo0_rs, halo1_ss, halo1_rs,
):
    me = lax.axis_index("ba")
    mine = lax.axis_index("ka")
    ring = lax.axis_size("ka")
    sides = (lax.rem(mine + 1, ring), lax.rem(mine + ring - 1, ring))

    loads = [
        pltpu.make_async_copy(a, b, load_sem.at[i])
        for i, (a, b) in enumerate(((dens_hbm, dens), (coup_hbm, coup), (h_hbm, hraw)))
    ]
    for load in loads:
        load.start()

    barrier = pltpu.get_barrier_semaphore()
    for i in range(1, GROUP):
        pl.semaphore_signal(
            barrier, inc=1, device_id={"ba": lax.rem(me + i, GROUP)}, device_id_type=MESH
        )
    for side in sides:
        pl.semaphore_signal(barrier, inc=1, device_id={"ka": side}, device_id_type=MESH)

    loads[0].wait()
    for t in range(2):
        cut = pl.ds(t * TILE, TILE)
        first, second = merge(dens[0, :, cut], dens[1, :, cut])
        low0[2 * t] = first.astype(BF16)
        low0[2 * t + 1] = second.astype(BF16)
        sigma[2 * t] = first
        sigma[2 * t + 1] = second

    pl.semaphore_wait(barrier, GROUP + 1)

    def halo0_copy(side):
        return pltpu.make_async_remote_copy(
            src_ref=low0,
            dst_ref=halo0.at[side],
            send_sem=halo0_ss.at[side],
            recv_sem=halo0_rs.at[side],
            device_id={"ka": sides[side]},
            device_id_type=MESH,
        )

    for side in range(2):
        halo0_copy(side).start()

    def enc_copy(phase, there, slot_s, slot_r):
        return pltpu.make_async_remote_copy(
            src_ref=enc_s.at[phase, slot_s],
            dst_ref=enc_r.at[phase, slot_r],
            send_sem=enc_ss.at[phase, slot_s],
            recv_sem=enc_rs.at[phase, slot_r],
            device_id={"ba": there},
            device_id_type=MESH,
        )

    def scale_copy(phase, there, slot_s, slot_r):
        return pltpu.make_async_remote_copy(
            src_ref=scale_s.at[phase, slot_s],
            dst_ref=scale_r.at[phase, slot_r],
            send_sem=scale_ss.at[phase, slot_s],
            recv_sem=scale_rs.at[phase, slot_r],
            device_id={"ba": there},
            device_id_type=MESH,
        )

    def send_all(phase, values_of):
        def step(i, carry):
            there = lax.rem(me + i, GROUP)
            codes, scale = encode(values_of(there))
            enc_s[phase, there] = codes
            scale_s[phase, there] = scale
            enc_copy(phase, there, there, me).start()
            scale_copy(phase, there, there, me).start()
            return carry

        lax.fori_loop(1, GROUP, step, 0)
        codes, scale = encode(values_of(me))
        enc_r[phase, me] = codes
        scale_r[phase, me] = scale

    def wait_from(phase, i):
        @pl.when(i > 0)
        def _():
            src = lax.rem(me + GROUP - i, GROUP)
            enc_copy(phase, src, src, src).wait_recv()
            scale_copy(phase, src, src, src).wait_recv()

    def momenta(block):
        return pl.ds(pl.multiple_of(block * GROUP, GROUP), GROUP)

    def rows(block):
        return pl.ds(pl.multiple_of(block * ROWS, ROWS), ROWS)

    def of_momenta(block):
        return sigma[:, momenta(block), :].reshape(ROWS, TILE)

    send_all(0, of_momenta)

    loads[1].wait()
    for t in range(2):
        tile = mine * 2 + t
        for position in range(2 + 2 * REACH):
            block = jnp.zeros((TILE, TILE), F32)
            if 0 <= position - t <= 2 * REACH:
                for s in range(ND):
                    offset = lax.rem(donors[t, s] - tile + REACH + TILES, TILES)
                    used = jnp.logical_and(offset == position - t, counts[t] > s)
                    weight = jnp.where(used, -1.0, 0.0).astype(F32)
                    block = block + coup[t, s].astype(F32) * weight
            mix[pl.ds(t * TILE, TILE), pl.ds(position * TILE, TILE)] = block.astype(BF16)

    loads[2].wait()

    def lay(t, carry):
        cut = pl.ds(pl.multiple_of(t * TILE, TILE), TILE)
        first, second = merge(hraw[0, :, cut], hraw[1, :, cut])
        base = pl.multiple_of(t * 2 * GROUP, 2 * GROUP)
        hband[pl.ds(base, GROUP), :] = first
        hband[pl.ds(base + GROUP, GROUP), :] = second
        return carry

    lax.fori_loop(0, NB // 2, lay, 0)

    def field(left, own, right):
        for a in range(4):
            total = jnp.zeros((2 * TILE, TILE), F32)
            for i, part in enumerate((left(a), own(a), right(a))):
                total += jnp.dot(
                    mix[:, pl.ds(i * 2 * TILE, 2 * TILE)], part, preferred_element_type=F32
                )
            sigma[a] = total

    for side in range(2):
        halo0_copy(side).wait_recv()
    field(lambda a: halo0[0, a], lambda a: low0[a], lambda a: halo0[1, a])
    send_all(1, of_momenta)

    def take_state(i, carry):
        wait_from(0, i)
        src = lax.rem(me + GROUP - i, GROUP)
        state[rows(src), :] = decode(enc_r[0, src], scale_r[0, src])
        return carry

    lax.fori_loop(0, GROUP, take_state, 0)

    def take_field(phase):
        def step(i, carry):
            wait_from(phase, i)
            src = lax.rem(me + GROUP - i, GROUP)
            ham[rows(src), :] = hband[rows(src), :] + decode(
                enc_r[phase, src], scale_r[phase, src]
            )
            return carry

        lax.fori_loop(0, GROUP, step, 0)

    take_field(1)

    def first_stage(m, carry):
        cut = pl.ds(m, NB, stride=GROUP)
        here = state[cut, :]
        state[cut, :] = here + (0.5 * step_size) * rate(ham[cut, :], here)
        return carry

    lax.fori_loop(0, GROUP, first_stage, 0)

    def mid_copy(there, slot_s, slot_r):
        return pltpu.make_async_remote_copy(
            src_ref=mid_s.at[slot_s],
            dst_ref=mid_r.at[slot_r],
            send_sem=mid_ss.at[slot_s],
            recv_sem=mid_rs.at[slot_r],
            device_id={"ba": there},
            device_id_type=MESH,
        )

    def send_mid(i, carry):
        there = lax.rem(me + i, GROUP)
        mid_s[there] = state[rows(there), :].astype(BF16)
        mid_copy(there, there, me).start()
        return carry

    lax.fori_loop(1, GROUP, send_mid, 0)
    mid_r[me] = state[rows(me), :].astype(BF16)

    def halo1_copy(side, slot):
        return pltpu.make_async_remote_copy(
            src_ref=mid_r.at[slot],
            dst_ref=halo1.at[side, slot],
            send_sem=halo1_ss.at[side, slot],
            recv_sem=halo1_rs.at[side, slot],
            device_id={"ka": sides[side]},
            device_id_type=MESH,
        )

    def forward(i, carry):
        src = lax.rem(me + GROUP - i, GROUP)

        @pl.when(i > 0)
        def _():
            mid_copy(src, src, src).wait_recv()

        for side in range(2):
            halo1_copy(side, src).start()
        return carry

    lax.fori_loop(0, GROUP, forward, 0)

    def halo1_in(i, carry):
        for side in range(2):
            halo1_copy(side, i).wait_recv()
        return carry

    lax.fori_loop(0, GROUP, halo1_in, 0)

    def band(ref, a):
        return ref[:, pl.ds(a * GROUP, GROUP), :].reshape(2 * TILE, TILE)

    field(
        lambda a: band(halo1.at[0], a), lambda a: band(mid_r, a), lambda a: band(halo1.at[1], a)
    )
    send_all(2, of_momenta)
    take_field(2)

    def second_stage(m, carry):
        cut = pl.ds(m, NB, stride=GROUP)
        rate_two[cut, :] = step_size * rate(ham[cut, :], state[cut, :])
        return carry

    lax.fori_loop(0, GROUP, second_stage, 0)
    send_all(3, lambda block: rate_two[rows(block), :])

    def out_copy(src):
        return pltpu.make_async_copy(
            out_v.at[:, momenta(src), :], out_hbm.at[:, momenta(src), :], out_sem.at[src]
        )

    def finish(i, carry):
        wait_from(3, i)
        src = lax.rem(me + GROUP - i, GROUP)
        change = decode(enc_r[3, src], scale_r[3, src])
        for t in range(2):
            base = t * 2 * GROUP
            real, imag = split(change[base : base + GROUP], change[base + GROUP : base + 2 * GROUP])
            cut = pl.ds(t * TILE, TILE)
            out_v[0, momenta(src), cut] = dens[0, momenta(src), cut] + real
            out_v[1, momenta(src), cut] = dens[1, momenta(src), cut] + imag
        out_copy(src).start()
        return carry

    lax.fori_loop(0, GROUP, finish, 0)

    for side in range(2):
        halo0_copy(side).wait_send()

    def drain(i, carry):
        there = lax.rem(me + i, GROUP)
        for phase in range(4):
            enc_copy(phase, there, there, me).wait_send()
            scale_copy(phase, there, there, me).wait_send()
        mid_copy(there, there, me).wait_send()
        return carry

    lax.fori_loop(1, GROUP, drain, 0)

    def drain_all(i, carry):
        for side in range(2):
            halo1_copy(side, i).wait_send()
        out_copy(i).wait()
        return carry

    lax.fori_loop(0, GROUP, drain_all, 0)


def local(density, h_bands, coupling, donors, counts):
    message = (GROUP, ROWS, TILE)
    big = (NB * GROUP, TILE)
    dma = pltpu.SemaphoreType.DMA
    anywhere = pl.BlockSpec(memory_space=pl.ANY)
    scalars = pl.BlockSpec(memory_space=pltpu.SMEM)
    return pl.pallas_call(
        kernel,
        out_shape=jax.ShapeDtypeStruct(density.shape, F32),
        in_specs=[anywhere, anywhere, anywhere, scalars, scalars],
        out_specs=anywhere,
        scratch_shapes=[
            pltpu.VMEM(density.shape, F32),
            pltpu.VMEM(h_bands.shape, F32),
            pltpu.VMEM(coupling.shape, BF16),
            pltpu.VMEM((4, 2 * TILE, TILE), BF16),
            pltpu.VMEM((2, 4, 2 * TILE, TILE), BF16),
            pltpu.VMEM((2 * TILE, 6 * TILE), BF16),
            pltpu.VMEM(big, F32),
            pltpu.VMEM(big, F32),
            pltpu.VMEM(big, F32),
            pltpu.VMEM(big, F32),
            pltpu.VMEM((4, 2 * TILE, TILE), F32),
            pltpu.VMEM((4, *message), I16),
            pltpu.VMEM((4, *message), I16),
            pltpu.VMEM((4, GROUP, 1, TILE), F32),
            pltpu.VMEM((4, GROUP, 1, TILE), F32),
            pltpu.VMEM(message, BF16),
            pltpu.VMEM(message, BF16),
            pltpu.VMEM((2, *message), BF16),
            pltpu.VMEM(density.shape, F32),
            dma((3,)),
            dma((GROUP,)),
            dma((4, GROUP)),
            dma((4, GROUP)),
            dma((4, GROUP)),
            dma((4, GROUP)),
            dma((GROUP,)),
            dma((GROUP,)),
            dma((2,)),
            dma((2,)),
            dma((2, GROUP)),
            dma((2, GROUP)),
        ],
        compiler_params=pltpu.CompilerParams(
            collective_id=0, has_side_effects=True, vmem_limit_bytes=40 << 20
        ),
    )(density, h_bands, coupling, donors, counts)


def solution(mesh):
    placed = (
        P(None, "ka", "ba"),
        P(None, ("ka", "ba"), None),
        P("ka", None, None, None),
        P("ka", None),
        P("ka"),
    )
    return jax.shard_map(
        local, mesh=mesh, in_specs=placed, out_specs=P(None, "ka", "ba"), check_vma=False
    )
```

```python
import jax
import jax.numpy as jnp
from jax import lax
from jax.experimental import pallas as pl
from jax.experimental.pallas import tpu as pltpu
from jax.sharding import PartitionSpec as P

NB = 64
TILE = 128
ND = 4
REACH = 2
TILES = 64
GROUP = 16
PART = 8
ROWS = 32
HALF = NB * PART
MESH = pl.DeviceIdType.MESH
F32, BF16, I16 = jnp.float32, jnp.bfloat16, jnp.int16
TOP = 32760.0

step_size = 0.25


def low_half(shape):
    return lax.broadcasted_iota(jnp.int32, shape, len(shape) - 1) < NB


def merge(real, imag):
    low = low_half(real.shape)
    first = jnp.where(low, real, pltpu.roll(imag, NB, 1))
    second = jnp.where(low, pltpu.roll(real, NB, 1), imag)
    return first, second


def split(first, second):
    low = low_half(first.shape)
    real = jnp.where(low, first, pltpu.roll(second, NB, 1))
    imag = jnp.where(low, pltpu.roll(first, NB, 1), second)
    return real, imag


def encode(*parts):
    top = parts[0][:1] * 0 + 1e-30
    for part in parts:
        top = jnp.maximum(top, jnp.max(jnp.abs(part), axis=0, keepdims=True))
    turn = TOP / top
    codes = [jnp.round(part * turn).astype(jnp.int32).astype(I16) for part in parts]
    return codes, top * (1.0 / TOP)


def decode(codes, scale):
    return codes.astype(jnp.int32).astype(F32) * scale


def halves(values):
    high = values.astype(BF16)
    return high, (values - high.astype(F32)).astype(BF16)


def rate(hamilton, state):
    sign = jnp.where(low_half(state.shape), 1.0, -1.0).astype(F32)
    turned_s = pltpu.roll(state, NB, 1) * sign
    turned_h = pltpu.roll(hamilton, NB, 1) * sign
    right_high, right_low = halves(
        jnp.concatenate([turned_s, state, turned_h, hamilton], axis=0)
    )
    left_high, left_low = halves(jnp.concatenate([hamilton, -state], axis=1))
    left = jnp.concatenate([left_high, left_low], axis=0)
    right = jnp.concatenate([right_high, right_low], axis=1)
    out = jnp.dot(left, right, preferred_element_type=F32)
    return out[:NB, :TILE] + (out[:NB, TILE:] + out[NB:, :TILE])


def kernel(
    dens_hbm, h_hbm, coup_hbm, donors_hbm, counts_hbm, out,
    dens, hraw, coup, donors, counts, low0, halo0, mix, hband, state, ham, change, sigma,
    whole_s, whole_r, enc_s, enc_r, scale_s, scale_r, mid_s, mid_r, halo1,
    load_sem, enc_ss, enc_rs, scale_ss, scale_rs, last_rs, last_scale_rs,
    mid_ss, mid_rs, halo0_ss, halo0_rs, halo1_ss, halo1_rs,
):
    me = lax.axis_index("ba")
    mine = lax.axis_index("ka")
    ring = lax.axis_size("ka")
    sides = (lax.rem(mine + 1, ring), lax.rem(mine + ring - 1, ring))

    pairs = (
        (dens_hbm, dens),
        (coup_hbm, coup),
        (h_hbm, hraw),
        (donors_hbm, donors),
        (counts_hbm, counts),
    )
    loads = [pltpu.make_async_copy(a, b, load_sem.at[i]) for i, (a, b) in enumerate(pairs)]
    for load in loads:
        load.start()

    barrier = pltpu.get_barrier_semaphore()
    for i in range(1, GROUP):
        pl.semaphore_signal(
            barrier, inc=1, device_id={"ba": lax.rem(me + i, GROUP)}, device_id_type=MESH
        )
    for side in sides:
        pl.semaphore_signal(barrier, inc=1, device_id={"ka": side}, device_id_type=MESH)

    def partner(i):
        step = (1 - 2 * lax.rem(i, 2)) * ((i + 1) // 2)
        return lax.rem(me + GROUP // 2 + step, GROUP)

    def to_ba(src, dst, send_sem, recv_sem, there):
        return pltpu.make_async_remote_copy(
            src_ref=src,
            dst_ref=dst,
            send_sem=send_sem,
            recv_sem=recv_sem,
            device_id={"ba": there},
            device_id_type=MESH,
        )

    def to_ka(src, dst, send_sem, recv_sem, side):
        return pltpu.make_async_remote_copy(
            src_ref=src,
            dst_ref=dst,
            send_sem=send_sem,
            recv_sem=recv_sem,
            device_id={"ka": sides[side]},
            device_id_type=MESH,
        )

    others = pl.ds(0, GROUP - 1)

    def codes_of(slot, sending, which):
        if slot == 0:
            return (whole_s if sending else whole_r).at[which]
        return (enc_s if sending else enc_r).at[slot - 1, which]

    def enc_copy(slot, there, group=None):
        return to_ba(
            codes_of(slot, True, there),
            codes_of(slot, False, me),
            enc_ss.at[slot],
            enc_rs.at[slot] if slot < 6 else last_rs.at[group],
            there,
        )

    def enc_all(slot, which=others, group=0):
        ref = codes_of(slot, False, which)
        recv_sem = enc_rs.at[slot] if slot < 6 else last_rs.at[group]
        return to_ba(ref, ref, enc_ss.at[slot], recv_sem, me)

    def scale_copy(slot, there, group=None):
        return to_ba(
            scale_s.at[slot, there],
            scale_r.at[slot, me],
            scale_ss.at[slot],
            scale_rs.at[slot] if slot < 6 else last_scale_rs.at[group],
            there,
        )

    def scale_all(slot, which=others, group=0):
        ref = scale_r.at[slot, which]
        recv_sem = scale_rs.at[slot] if slot < 6 else last_scale_rs.at[group]
        return to_ba(ref, ref, scale_ss.at[slot], recv_sem, me)

    def halo0_copy(side, chunk):
        cut = pl.ds(2 * chunk, 2)
        return to_ka(
            low0.at[cut],
            halo0.at[side, cut],
            halo0_ss.at[side, chunk],
            halo0_rs.at[side, chunk],
            side,
        )

    def mid_copy(chunk, there, group):
        return to_ba(
            mid_s.at[chunk, there],
            mid_r.at[chunk, me],
            mid_ss.at[chunk],
            mid_rs.at[chunk, group],
            there,
        )

    def mid_group(chunk, which, group):
        ref = mid_r.at[chunk, which]
        return to_ba(ref, ref, mid_ss.at[chunk], mid_rs.at[chunk, group], me)

    def halo1_copy(side, chunk, src):
        return to_ka(
            mid_r.at[chunk, src],
            halo1.at[side, chunk, src],
            halo1_ss.at[side, chunk],
            halo1_rs.at[side, chunk],
            side,
        )

    def halo1_all(side, chunk):
        ref = halo1.at[side, chunk]
        return to_ka(ref, ref, halo1_ss.at[side, chunk], halo1_rs.at[side, chunk], side)

    def momenta(block, half):
        return pl.ds(pl.multiple_of(block * GROUP + half * PART, PART), PART)

    def rows(half, block):
        return pl.ds(pl.multiple_of(half * HALF + block * ROWS, ROWS), ROWS)

    def parts_of(there):
        return [sigma[:, momenta(there, half), :].reshape(ROWS, TILE) for half in range(2)]

    def by_partner(put, start, near=False):
        def body(n, carry):
            order = [GROUP - 2 - 3 * n - i if near else 3 * n + i for i in range(3)]
            for i in order:
                put(i, partner(i))
            for i in order:
                start(i, partner(i))
            return carry

        lax.fori_loop(0, (GROUP - 1) // 3, body, 0)

    def send_codes(slot, put, group=False):
        def start(i, there):
            of = (i + 1) // 2 if group else None
            enc_copy(slot, there, of).start()
            scale_copy(slot, there, of).start()

        sending = whole_s if slot == 0 else enc_s
        by_partner(lambda i, there: put(sending, scale_s, there, there), start)
        put(whole_r if slot == 0 else enc_r, scale_r, me, me)

    loads[0].wait()
    for t in range(2):
        cut = pl.ds(t * TILE, TILE)
        for a, values in zip((2 * t, 2 * t + 1), merge(dens[0, :, cut], dens[1, :, cut])):
            low0[a] = values.astype(BF16)
            sigma[a] = values
        if t == 0:
            pl.semaphore_wait(barrier, GROUP + 1)
        for side in range(2):
            halo0_copy(side, t).start()

    def put_whole(codes_ref, scale_ref, slot, there):
        codes, scale = encode(*parts_of(there))
        for half in range(2):
            codes_ref[slot, pl.ds(half * ROWS, ROWS), :] = codes[half]
        scale_ref[0, slot] = scale

    send_codes(0, put_whole)

    for load in (loads[1], loads[3], loads[4]):
        load.wait()
    for t in range(2):
        tile = mine * 2 + t
        for position in range(2 + 2 * REACH):
            block = jnp.zeros((TILE, TILE), F32)
            if 0 <= position - t <= 2 * REACH:
                for s in range(ND):
                    offset = lax.rem(donors[t, s] - tile + REACH + TILES, TILES)
                    used = jnp.logical_and(offset == position - t, counts[t] > s)
                    weight = jnp.where(used, -1.0, 0.0).astype(F32)
                    block = block + coup[t, s].astype(F32) * weight
            mix[pl.ds(t * TILE, TILE), pl.ds(position * TILE, TILE)] = block.astype(BF16)

    def mixed(block, values):
        cut = pl.ds(block * 2 * TILE, 2 * TILE)
        return jnp.dot(mix[:, cut], values, preferred_element_type=F32)

    for a in range(4):
        sigma[a] = mixed(1, low0[a])

    loads[2].wait()

    def lay(step, carry):
        for i in range(4):
            t = step * 4 + i
            cut = pl.ds(pl.multiple_of(t * TILE, TILE), TILE)
            for half in range(2):
                part = pl.ds(half * PART, PART)
                first, second = merge(hraw[0, part, cut], hraw[1, part, cut])
                base = pl.multiple_of(half * HALF + t * 2 * PART, 2 * PART)
                hband[pl.ds(base, PART), :] = first
                hband[pl.ds(base + PART, PART), :] = second
        return carry

    lax.fori_loop(0, NB // 8, lay, 0)

    def send_bands(first_slot, chunk):
        slot, bands = first_slot + chunk, pl.ds(2 * chunk, 2)

        def put(codes_ref, scale_ref, index, there):
            parts = [
                sigma[bands, momenta(there, half), :].reshape(ROWS // 2, TILE) for half in range(2)
            ]
            codes, scale = encode(*parts)
            for half in range(2):
                codes_ref[slot - 1, index, pl.ds(half * ROWS // 2, ROWS // 2), :] = codes[half]
            scale_ref[slot, index] = scale

        send_codes(slot, put)

    def take_bands(first_slot, chunk):
        slot = first_slot + chunk
        scale_all(slot).wait_recv()
        enc_all(slot).wait_recv()

        def take(src, carry):
            values = decode(enc_r[slot - 1, src], scale_r[slot, src])
            for half in range(2):
                base = half * HALF + src * ROWS + chunk * ROWS // 2
                cut = pl.ds(pl.multiple_of(base, ROWS // 2), ROWS // 2)
                ham[cut, :] = hband[cut, :] + values[half * ROWS // 2 : (half + 1) * ROWS // 2]
            return carry

        lax.fori_loop(0, GROUP, take, 0)

    for chunk in range(2):
        for side in range(2):
            halo0_copy(side, chunk).wait_recv()
        for a in (2 * chunk, 2 * chunk + 1):
            sigma[a] += mixed(0, halo0[0, a]) + mixed(2, halo0[1, a])
        send_bands(1, chunk)

    scale_all(0).wait_recv()
    enc_all(0).wait_recv()

    def take_state(src, carry):
        values = decode(whole_r[src], scale_r[0, src])
        for half in range(2):
            state[rows(half, src), :] = values[half * ROWS : (half + 1) * ROWS]
        return carry

    lax.fori_loop(0, GROUP, take_state, 0)

    for chunk in range(2):
        take_bands(1, chunk)

    def each_momentum(half, use):
        def step(quad, carry):
            cuts = [pl.ds(half * HALF + quad * 4 + i, NB, stride=PART) for i in range(4)]
            states = [state[cut, :] for cut in cuts]
            rates = [rate(ham[cut, :], here) for cut, here in zip(cuts, states)]
            for cut, here, gained in zip(cuts, states, rates):
                use(cut, here, gained)
            return carry

        lax.fori_loop(0, 2, step, 0)

    def to_middle(cut, here, gained):
        state[cut, :] = here + (0.5 * step_size) * gained

    def to_change(cut, here, gained):
        change[cut, :] = step_size * gained

    for half in range(2):
        each_momentum(half, to_middle)

    def middle_of(chunk, there):
        parts = []
        for half in range(2):
            base = half * HALF + there * ROWS + chunk * ROWS // 2
            cut = pl.ds(pl.multiple_of(base, ROWS // 2), ROWS // 2)
            parts.append(state[cut, :].reshape(2, PART, TILE))
        return jnp.concatenate(parts, axis=1).astype(BF16)

    for chunk in range(2):

        def put_mid(i, there, chunk=chunk):
            mid_s[chunk, there] = middle_of(chunk, there)

        def start_mid(i, there, chunk=chunk):
            mid_copy(chunk, there, (i + 1) // 2).start()

        by_partner(put_mid, start_mid, near=True)
        mid_r[chunk, me] = middle_of(chunk, me)

    for chunk in range(2):
        for side in range(2):
            halo1_copy(side, chunk, me).start()

        def forward(group, members, chunk=chunk):
            mid_group(chunk, pl.ds(0, len(members)), group).wait_recv()
            for i in members:
                for side in range(2):
                    halo1_copy(side, chunk, partner(i)).start()

        def forward_pair(n, carry, forward=forward):
            group = GROUP // 2 - n
            forward(group, [2 * group, 2 * group - 1])
            return carry

        lax.fori_loop(1, GROUP // 2, forward_pair, 0)
        forward(0, [0])

    def band(ref, chunk, i):
        return ref[chunk, :, i].reshape(2 * TILE, TILE)

    for chunk in range(2):
        for i in range(2):
            sigma[2 * chunk + i] = mixed(1, band(mid_r, chunk, i))
    for chunk in range(2):
        for side in range(2):
            halo1_all(side, chunk).wait_recv()
        for i in range(2):
            left, right = (band(halo1.at[side], chunk, i) for side in range(2))
            sigma[2 * chunk + i] += mixed(0, left) + mixed(2, right)
        send_bands(3, chunk)

    for chunk in range(2):
        take_bands(3, chunk)

    for half in range(2):
        each_momentum(half, to_change)

        def put_change(codes_ref, scale_ref, index, there, half=half):
            (codes,), scale = encode(change[rows(half, there), :])
            codes_ref[4 + half, index] = codes
            scale_ref[5 + half, index] = scale

        send_codes(5 + half, put_change, group=True)

    for chunk in range(2):
        for side in range(2):
            halo0_copy(side, chunk).wait_send()
            halo1_all(side, chunk).wait_send()
        mid_group(chunk, others, 0).wait_send()
    for slot in range(5):
        enc_all(slot).wait_send()
        scale_all(slot).wait_send()

    def finish(half, sources):
        done = []
        for src in sources:
            gained = decode(enc_r[4 + half, src], scale_r[5 + half, src])
            part = momenta(src, half)
            for t in range(2):
                base = t * 2 * PART
                first, second = gained[base : base + PART], gained[base + PART : base + 2 * PART]
                cut = pl.ds(t * TILE, TILE)
                for c, change_c in enumerate(split(first, second)):
                    done.append((c, part, cut, dens[c, part, cut] + change_c))
        for c, part, cut, values in done:
            out[c, part, cut] = values

    scale_all(5).wait_recv()
    enc_all(5).wait_recv()

    def finish_first(step, carry):
        finish(0, [step * 4 + i for i in range(4)])
        return carry

    lax.fori_loop(0, GROUP // 4, finish_first, 0)
    finish(1, [me])

    def finish_group(group, members):
        which = pl.ds(0, len(members))
        enc_all(6, which, group).wait_recv()
        scale_all(6, which, group).wait_recv()
        finish(1, [partner(i) for i in members])

    finish_group(0, [0])

    def finish_pair(group, carry):
        finish_group(group, [2 * group - 1, 2 * group])
        return carry

    lax.fori_loop(1, GROUP // 2, finish_pair, 0)
    for slot in (5, 6):
        enc_all(slot).wait_send()
        scale_all(slot).wait_send()


def local(density, h_bands, coupling, donors, counts):
    whole = (GROUP, 2 * ROWS, TILE)
    codes = (6, GROUP, ROWS, TILE)
    scales = (7, GROUP, 1, TILE)
    middle = (2, GROUP, 2, GROUP, TILE)
    big = (NB * GROUP, TILE)
    dma = pltpu.SemaphoreType.DMA
    anywhere = pl.BlockSpec(memory_space=pl.ANY)
    operands = [
        pltpu.with_memory_space_constraint(x, pltpu.HBM)
        for x in (density, h_bands, coupling, donors, counts)
    ]
    return pl.pallas_call(
        kernel,
        out_shape=pltpu.VMEM(density.shape, F32),
        in_specs=[anywhere] * 5,
        out_specs=pl.BlockSpec(memory_space=pltpu.VMEM),
        scratch_shapes=[
            pltpu.VMEM(density.shape, F32),
            pltpu.VMEM(h_bands.shape, F32),
            pltpu.VMEM(coupling.shape, BF16),
            pltpu.SMEM(donors.shape, jnp.int32),
            pltpu.SMEM(counts.shape, jnp.int32),
            pltpu.VMEM((4, 2 * TILE, TILE), BF16),
            pltpu.VMEM((2, 4, 2 * TILE, TILE), BF16),
            pltpu.VMEM((2 * TILE, 6 * TILE), BF16),
            pltpu.VMEM(big, F32),
            pltpu.VMEM(big, F32),
            pltpu.VMEM(big, F32),
            pltpu.VMEM(big, F32),
            pltpu.VMEM((4, 2 * TILE, TILE), F32),
            pltpu.VMEM(whole, I16),
            pltpu.VMEM(whole, I16),
            pltpu.VMEM(codes, I16),
            pltpu.VMEM(codes, I16),
            pltpu.VMEM(scales, F32),
            pltpu.VMEM(scales, F32),
            pltpu.VMEM(middle, BF16),
            pltpu.VMEM(middle, BF16),
            pltpu.VMEM((2, *middle), BF16),
            dma((5,)),
            dma((7,)),
            dma((6,)),
            dma((7,)),
            dma((6,)),
            dma((GROUP // 2,)),
            dma((GROUP // 2,)),
            dma((2,)),
            dma((2, GROUP // 2)),
            dma((2, 2)),
            dma((2, 2)),
            dma((2, 2)),
            dma((2, 2)),
        ],
        compiler_params=pltpu.CompilerParams(
            collective_id=0, has_side_effects=True, vmem_limit_bytes=40 << 20
        ),
    )(*operands)


def solution(mesh):
    placed = (
        P(None, "ka", "ba"),
        P(None, ("ka", "ba"), None),
        P("ka", None, None, None),
        P("ka", None),
        P("ka"),
    )
    return jax.shard_map(
        local, mesh=mesh, in_specs=placed, out_specs=P(None, "ka", "ba"), check_vma=False
    )
```

```python
import jax
import jax.numpy as jnp
from jax import lax
from jax.experimental import pallas as pl
from jax.experimental.pallas import tpu as pltpu
from jax.sharding import PartitionSpec as P

NB = 64
TILE = 128
ND = 4
REACH = 2
TILES = 64
GROUP = 16
PART = 8
ROWS = 32
HALF = NB * PART
MESH = pl.DeviceIdType.MESH
F32, BF16, I16 = jnp.float32, jnp.bfloat16, jnp.int16
TOP = 32760.0

step_size = 0.25


def low_half(shape):
    return lax.broadcasted_iota(jnp.int32, shape, len(shape) - 1) < NB


def merge(real, imag):
    low = low_half(real.shape)
    first = jnp.where(low, real, pltpu.roll(imag, NB, 1))
    second = jnp.where(low, pltpu.roll(real, NB, 1), imag)
    return first, second


def split(first, second):
    low = low_half(first.shape)
    real = jnp.where(low, first, pltpu.roll(second, NB, 1))
    imag = jnp.where(low, pltpu.roll(first, NB, 1), second)
    return real, imag


def encode(*parts):
    top = parts[0][:1] * 0 + 1e-30
    for part in parts:
        top = jnp.maximum(top, jnp.max(jnp.abs(part), axis=0, keepdims=True))
    turn = TOP / top
    codes = [jnp.round(part * turn).astype(jnp.int32).astype(I16) for part in parts]
    return codes, top * (1.0 / TOP)


def decode(codes, scale):
    return codes.astype(jnp.int32).astype(F32) * scale


def halves(values):
    high = values.astype(BF16)
    return high, (values - high.astype(F32)).astype(BF16)


def rate(hamilton, state):
    sign = jnp.where(low_half(state.shape), 1.0, -1.0).astype(F32)
    turned_s = pltpu.roll(state, NB, 1) * sign
    turned_h = pltpu.roll(hamilton, NB, 1) * sign
    right_high, right_low = halves(
        jnp.concatenate([turned_s, state, turned_h, hamilton], axis=0)
    )
    left_high, left_low = halves(jnp.concatenate([hamilton, -state], axis=1))
    left = jnp.concatenate([left_high, left_low], axis=0)
    right = jnp.concatenate([right_high, right_low], axis=1)
    out = jnp.dot(left, right, preferred_element_type=F32)
    return out[:NB, :TILE] + (out[:NB, TILE:] + out[NB:, :TILE])


def kernel(
    dens_hbm, h_hbm, coup_hbm, donors_hbm, counts_hbm, out,
    dens, hraw, coup, donors, counts, low0, halo0, mix, hband, state, ham, change, sigma,
    whole_s, whole_r, enc_s, enc_r, scale_s, scale_r, mid_s, mid_r, halo1,
    load_sem, enc_ss, enc_rs, scale_ss, scale_rs, last_rs, last_scale_rs,
    mid_ss, mid_rs, halo0_ss, halo0_rs, halo1_ss, halo1_rs,
):
    me = lax.axis_index("ba")
    mine = lax.axis_index("ka")
    ring = lax.axis_size("ka")
    sides = (lax.rem(mine + 1, ring), lax.rem(mine + ring - 1, ring))

    pairs = (
        (dens_hbm, dens),
        (coup_hbm, coup),
        (h_hbm, hraw),
        (donors_hbm, donors),
        (counts_hbm, counts),
    )
    loads = [pltpu.make_async_copy(a, b, load_sem.at[i]) for i, (a, b) in enumerate(pairs)]
    for load in loads:
        load.start()

    barrier = pltpu.get_barrier_semaphore()
    for i in range(1, GROUP):
        pl.semaphore_signal(
            barrier, inc=1, device_id={"ba": lax.rem(me + i, GROUP)}, device_id_type=MESH
        )
    for side in sides:
        pl.semaphore_signal(barrier, inc=1, device_id={"ka": side}, device_id_type=MESH)

    def partner(i):
        step = (1 - 2 * lax.rem(i, 2)) * ((i + 1) // 2)
        return lax.rem(me + GROUP // 2 + step, GROUP)

    def to_ba(src, dst, send_sem, recv_sem, there):
        return pltpu.make_async_remote_copy(
            src_ref=src,
            dst_ref=dst,
            send_sem=send_sem,
            recv_sem=recv_sem,
            device_id={"ba": there},
            device_id_type=MESH,
        )

    def to_ka(src, dst, send_sem, recv_sem, side):
        return pltpu.make_async_remote_copy(
            src_ref=src,
            dst_ref=dst,
            send_sem=send_sem,
            recv_sem=recv_sem,
            device_id={"ka": sides[side]},
            device_id_type=MESH,
        )

    others = pl.ds(0, GROUP - 1)

    def codes_of(slot, sending, which, half):
        if slot == 0:
            return (whole_s if sending else whole_r).at[which]
        ref = enc_s if sending else enc_r
        if half is None:
            return ref.at[slot - 1, which]
        return ref.at[slot - 1, which, pl.ds(half * ROWS // 2, ROWS // 2)]

    def enc_sems(slot, half, group):
        of = slot // 2 + 6 if half == 1 else slot
        return enc_ss.at[of], last_rs.at[group] if slot == 6 else enc_rs.at[of]

    def enc_copy(slot, there, group=None, half=None):
        return to_ba(
            codes_of(slot, True, there, half),
            codes_of(slot, False, me, half),
            *enc_sems(slot, half, group),
            there,
        )

    def enc_all(slot, which=others, group=0, half=None):
        ref = codes_of(slot, False, which, half)
        return to_ba(ref, ref, *enc_sems(slot, half, group), me)

    def scale_copy(slot, there, group=None):
        return to_ba(
            scale_s.at[slot, there],
            scale_r.at[slot, me],
            scale_ss.at[slot],
            scale_rs.at[slot] if slot < 6 else last_scale_rs.at[group],
            there,
        )

    def scale_all(slot, which=others, group=0):
        ref = scale_r.at[slot, which]
        recv_sem = scale_rs.at[slot] if slot < 6 else last_scale_rs.at[group]
        return to_ba(ref, ref, scale_ss.at[slot], recv_sem, me)

    def halo0_copy(side, chunk):
        cut = pl.ds(2 * chunk, 2)
        return to_ka(
            low0.at[cut],
            halo0.at[side, cut],
            halo0_ss.at[side, chunk],
            halo0_rs.at[side, chunk],
            side,
        )

    def mid_copy(chunk, there, group):
        return to_ba(
            mid_s.at[chunk, there],
            mid_r.at[chunk, me],
            mid_ss.at[chunk],
            mid_rs.at[chunk, group],
            there,
        )

    def mid_group(chunk, which, group):
        ref = mid_r.at[chunk, which]
        return to_ba(ref, ref, mid_ss.at[chunk], mid_rs.at[chunk, group], me)

    def halo1_copy(side, chunk, src):
        return to_ka(
            mid_r.at[chunk, src],
            halo1.at[side, chunk, src],
            halo1_ss.at[side, chunk],
            halo1_rs.at[side, chunk],
            side,
        )

    def halo1_all(side, chunk):
        ref = halo1.at[side, chunk]
        return to_ka(ref, ref, halo1_ss.at[side, chunk], halo1_rs.at[side, chunk], side)

    def momenta(block, half):
        return pl.ds(pl.multiple_of(block * GROUP + half * PART, PART), PART)

    def rows(half, block):
        return pl.ds(pl.multiple_of(half * HALF + block * ROWS, ROWS), ROWS)

    def parts_of(there):
        return [sigma[:, momenta(there, half), :].reshape(ROWS, TILE) for half in range(2)]

    def by_partner(put, start, near=False):
        def body(n, carry):
            order = [GROUP - 2 - 3 * n - i if near else 3 * n + i for i in range(3)]
            for i in order:
                put(i, partner(i))
            for i in order:
                start(i, partner(i))
            return carry

        lax.fori_loop(0, (GROUP - 1) // 3, body, 0)

    def send_codes(slot, put, group=False, halves_apart=False):
        def start(i, there):
            of = (i + 1) // 2 if group else None
            enc_copy(slot, there, of, 0 if halves_apart else None).start()
            scale_copy(slot, there, of).start()

        sending = whole_s if slot == 0 else enc_s
        by_partner(lambda i, there: put(sending, scale_s, there, there), start)
        if halves_apart:
            by_partner(
                lambda i, there: None, lambda i, there: enc_copy(slot, there, None, 1).start()
            )
        put(whole_r if slot == 0 else enc_r, scale_r, me, me)

    loads[0].wait()
    for t in range(2):
        cut = pl.ds(t * TILE, TILE)
        for a, values in zip((2 * t, 2 * t + 1), merge(dens[0, :, cut], dens[1, :, cut])):
            low0[a] = values.astype(BF16)
            sigma[a] = values
        if t == 0:
            pl.semaphore_wait(barrier, GROUP + 1)
        for side in range(2):
            halo0_copy(side, t).start()

    def put_whole(codes_ref, scale_ref, slot, there):
        codes, scale = encode(*parts_of(there))
        for half in range(2):
            codes_ref[slot, pl.ds(half * ROWS, ROWS), :] = codes[half]
        scale_ref[0, slot] = scale

    send_codes(0, put_whole)

    for load in (loads[1], loads[3], loads[4]):
        load.wait()
    for t in range(2):
        tile = mine * 2 + t
        for position in range(2 + 2 * REACH):
            block = jnp.zeros((TILE, TILE), F32)
            if 0 <= position - t <= 2 * REACH:
                for s in range(ND):
                    offset = lax.rem(donors[t, s] - tile + REACH + TILES, TILES)
                    used = jnp.logical_and(offset == position - t, counts[t] > s)
                    weight = jnp.where(used, -1.0, 0.0).astype(F32)
                    block = block + coup[t, s].astype(F32) * weight
            mix[pl.ds(t * TILE, TILE), pl.ds(position * TILE, TILE)] = block.astype(BF16)

    def mixed(block, values):
        cut = pl.ds(block * 2 * TILE, 2 * TILE)
        return jnp.dot(mix[:, cut], values, preferred_element_type=F32)

    for a in range(4):
        sigma[a] = mixed(1, low0[a])

    loads[2].wait()

    def lay(step, carry):
        for i in range(4):
            t = step * 4 + i
            cut = pl.ds(pl.multiple_of(t * TILE, TILE), TILE)
            for half in range(2):
                part = pl.ds(half * PART, PART)
                first, second = merge(hraw[0, part, cut], hraw[1, part, cut])
                base = pl.multiple_of(half * HALF + t * 2 * PART, 2 * PART)
                hband[pl.ds(base, PART), :] = first
                hband[pl.ds(base + PART, PART), :] = second
        return carry

    lax.fori_loop(0, NB // 8, lay, 0)

    def send_bands(first_slot, chunk):
        slot, bands = first_slot + chunk, pl.ds(2 * chunk, 2)

        def put(codes_ref, scale_ref, index, there):
            parts = [
                sigma[bands, momenta(there, half), :].reshape(ROWS // 2, TILE) for half in range(2)
            ]
            codes, scale = encode(*parts)
            for half in range(2):
                codes_ref[slot - 1, index, pl.ds(half * ROWS // 2, ROWS // 2), :] = codes[half]
            scale_ref[slot, index] = scale

        send_codes(slot, put, halves_apart=chunk == 1)

    def take_bands(first_slot, chunk, half=None):
        slot = first_slot + chunk
        if half != 1:
            scale_all(slot).wait_recv()
        enc_all(slot, half=half).wait_recv()
        size = ROWS // 2

        def take(src, carry):
            for h in range(2) if half is None else (half,):
                part = enc_r[slot - 1, src, pl.ds(h * size, size), :]
                base = h * HALF + src * ROWS + chunk * size
                cut = pl.ds(pl.multiple_of(base, size), size)
                ham[cut, :] = hband[cut, :] + decode(part, scale_r[slot, src])
            return carry

        lax.fori_loop(0, GROUP, take, 0)

    for chunk in range(2):
        for side in range(2):
            halo0_copy(side, chunk).wait_recv()
        for a in (2 * chunk, 2 * chunk + 1):
            sigma[a] += mixed(0, halo0[0, a]) + mixed(2, halo0[1, a])
        send_bands(1, chunk)

    scale_all(0).wait_recv()
    enc_all(0).wait_recv()

    def take_state(src, carry):
        values = decode(whole_r[src], scale_r[0, src])
        for half in range(2):
            state[rows(half, src), :] = values[half * ROWS : (half + 1) * ROWS]
        return carry

    lax.fori_loop(0, GROUP, take_state, 0)

    take_bands(1, 0)

    def each_momentum(half, use):
        def step(quad, carry):
            cuts = [pl.ds(half * HALF + quad * 4 + i, NB, stride=PART) for i in range(4)]
            states = [state[cut, :] for cut in cuts]
            rates = [rate(ham[cut, :], here) for cut, here in zip(cuts, states)]
            for cut, here, gained in zip(cuts, states, rates):
                use(cut, here, gained)
            return carry

        lax.fori_loop(0, 2, step, 0)

    def to_middle(cut, here, gained):
        state[cut, :] = here + (0.5 * step_size) * gained

    def to_change(cut, here, gained):
        change[cut, :] = step_size * gained

    for half in range(2):
        take_bands(1, 1, half)
        each_momentum(half, to_middle)

    def middle_of(chunk, there):
        parts = []
        for half in range(2):
            base = half * HALF + there * ROWS + chunk * ROWS // 2
            cut = pl.ds(pl.multiple_of(base, ROWS // 2), ROWS // 2)
            parts.append(state[cut, :].reshape(2, PART, TILE))
        return jnp.concatenate(parts, axis=1).astype(BF16)

    for chunk in range(2):

        def put_mid(i, there, chunk=chunk):
            mid_s[chunk, there] = middle_of(chunk, there)

        def start_mid(i, there, chunk=chunk):
            mid_copy(chunk, there, (i + 1) // 2).start()

        by_partner(put_mid, start_mid, near=True)
        mid_r[chunk, me] = middle_of(chunk, me)

    for chunk in range(2):
        for side in range(2):
            halo1_copy(side, chunk, me).start()

    def forward(chunk, group):
        members = [2 * group, 2 * group - 1] if group > 0 else [0]
        mid_group(chunk, pl.ds(0, len(members)), group).wait_recv()
        for i in members:
            for side in range(2):
                halo1_copy(side, chunk, partner(i)).start()

    for group in (7, 6, 5):
        forward(0, group)
    for group in (4, 3, 2, 1, 0):
        forward(0, group)
        forward(1, group + 3)
    for group in (2, 1, 0):
        forward(1, group)

    def band(ref, chunk, i):
        return ref[chunk, :, i].reshape(2 * TILE, TILE)

    for chunk in range(2):
        for i in range(2):
            sigma[2 * chunk + i] = mixed(1, band(mid_r, chunk, i))
    for chunk in range(2):
        for side in range(2):
            halo1_all(side, chunk).wait_recv()
        for i in range(2):
            left, right = (band(halo1.at[side], chunk, i) for side in range(2))
            sigma[2 * chunk + i] += mixed(0, left) + mixed(2, right)
        send_bands(3, chunk)

    take_bands(3, 0)
    for half in range(2):
        take_bands(3, 1, half)
        each_momentum(half, to_change)

        def put_change(codes_ref, scale_ref, index, there, half=half):
            (codes,), scale = encode(change[rows(half, there), :])
            codes_ref[4 + half, index] = codes
            scale_ref[5 + half, index] = scale

        send_codes(5 + half, put_change, group=True)

    for chunk in range(2):
        for side in range(2):
            halo0_copy(side, chunk).wait_send()
            halo1_all(side, chunk).wait_send()
        mid_group(chunk, others, 0).wait_send()
    for slot in range(5):
        for half in (0, 1) if slot in (2, 4) else (None,):
            enc_all(slot, half=half).wait_send()
        scale_all(slot).wait_send()

    def finish(half, sources):
        done = []
        for src in sources:
            gained = decode(enc_r[4 + half, src], scale_r[5 + half, src])
            part = momenta(src, half)
            for t in range(2):
                base = t * 2 * PART
                first, second = gained[base : base + PART], gained[base + PART : base + 2 * PART]
                cut = pl.ds(t * TILE, TILE)
                for c, change_c in enumerate(split(first, second)):
                    done.append((c, part, cut, dens[c, part, cut] + change_c))
        for c, part, cut, values in done:
            out[c, part, cut] = values

    scale_all(5).wait_recv()
    enc_all(5).wait_recv()

    def finish_first(step, carry):
        finish(0, [step * 4 + i for i in range(4)])
        return carry

    lax.fori_loop(0, GROUP // 4, finish_first, 0)
    finish(1, [me])

    def finish_group(group, members):
        which = pl.ds(0, len(members))
        enc_all(6, which, group).wait_recv()
        scale_all(6, which, group).wait_recv()
        finish(1, [partner(i) for i in members])

    finish_group(0, [0])

    def finish_pair(group, carry):
        finish_group(group, [2 * group - 1, 2 * group])
        return carry

    lax.fori_loop(1, GROUP // 2, finish_pair, 0)
    for slot in (5, 6):
        enc_all(slot).wait_send()
        scale_all(slot).wait_send()


def local(density, h_bands, coupling, donors, counts):
    whole = (GROUP, 2 * ROWS, TILE)
    codes = (6, GROUP, ROWS, TILE)
    scales = (7, GROUP, 1, TILE)
    middle = (2, GROUP, 2, GROUP, TILE)
    big = (NB * GROUP, TILE)
    dma = pltpu.SemaphoreType.DMA
    anywhere = pl.BlockSpec(memory_space=pl.ANY)
    operands = [
        pltpu.with_memory_space_constraint(x, pltpu.HBM)
        for x in (density, h_bands, coupling, donors, counts)
    ]
    return pl.pallas_call(
        kernel,
        out_shape=pltpu.VMEM(density.shape, F32),
        in_specs=[anywhere] * 5,
        out_specs=pl.BlockSpec(memory_space=pltpu.VMEM),
        scratch_shapes=[
            pltpu.VMEM(density.shape, F32),
            pltpu.VMEM(h_bands.shape, F32),
            pltpu.VMEM(coupling.shape, BF16),
            pltpu.SMEM(donors.shape, jnp.int32),
            pltpu.SMEM(counts.shape, jnp.int32),
            pltpu.VMEM((4, 2 * TILE, TILE), BF16),
            pltpu.VMEM((2, 4, 2 * TILE, TILE), BF16),
            pltpu.VMEM((2 * TILE, 6 * TILE), BF16),
            pltpu.VMEM(big, F32),
            pltpu.VMEM(big, F32),
            pltpu.VMEM(big, F32),
            pltpu.VMEM(big, F32),
            pltpu.VMEM((4, 2 * TILE, TILE), F32),
            pltpu.VMEM(whole, I16),
            pltpu.VMEM(whole, I16),
            pltpu.VMEM(codes, I16),
            pltpu.VMEM(codes, I16),
            pltpu.VMEM(scales, F32),
            pltpu.VMEM(scales, F32),
            pltpu.VMEM(middle, BF16),
            pltpu.VMEM(middle, BF16),
            pltpu.VMEM((2, *middle), BF16),
            dma((5,)),
            dma((9,)),
            dma((9,)),
            dma((7,)),
            dma((6,)),
            dma((GROUP // 2,)),
            dma((GROUP // 2,)),
            dma((2,)),
            dma((2, GROUP // 2)),
            dma((2, 2)),
            dma((2, 2)),
            dma((2, 2)),
            dma((2, 2)),
        ],
        compiler_params=pltpu.CompilerParams(
            collective_id=0, has_side_effects=True, vmem_limit_bytes=40 << 20
        ),
    )(*operands)


def solution(mesh):
    placed = (
        P(None, "ka", "ba"),
        P(None, ("ka", "ba"), None),
        P("ka", None, None, None),
        P("ka", None),
        P("ka"),
    )
    return jax.shard_map(
        local, mesh=mesh, in_specs=placed, out_specs=P(None, "ka", "ba"), check_vma=False
    )
```

```python
import jax
import jax.numpy as jnp
from jax import lax
from jax.experimental import pallas as pl
from jax.experimental.pallas import tpu as pltpu
from jax.sharding import PartitionSpec as P

NB = 64
TILE = 128
ND = 4
REACH = 2
TILES = 64
GROUP = 16
PART = 8
ROWS = 32
HALF = NB * PART
QUAD = 4
QUAD_ROWS = 4 * QUAD
MESH = pl.DeviceIdType.MESH
F32, BF16, I16 = jnp.float32, jnp.bfloat16, jnp.int16
TOP = 32760.0

step_size = 0.25


def low_half(shape):
    return lax.broadcasted_iota(jnp.int32, shape, len(shape) - 1) < NB


def merge(real, imag):
    low = low_half(real.shape)
    first = jnp.where(low, real, pltpu.roll(imag, NB, 1))
    second = jnp.where(low, pltpu.roll(real, NB, 1), imag)
    return first, second


def split(first, second):
    low = low_half(first.shape)
    real = jnp.where(low, first, pltpu.roll(second, NB, 1))
    imag = jnp.where(low, pltpu.roll(first, NB, 1), second)
    return real, imag


def encode(*parts):
    top = parts[0][:1] * 0 + 1e-30
    for part in parts:
        top = jnp.maximum(top, jnp.max(jnp.abs(part), axis=0, keepdims=True))
    turn = TOP / top
    codes = [jnp.round(part * turn).astype(jnp.int32).astype(I16) for part in parts]
    return codes, top * (1.0 / TOP)


def decode(codes, scale):
    return codes.astype(jnp.int32).astype(F32) * scale


def halves(values):
    high = values.astype(BF16)
    return high, (values - high.astype(F32)).astype(BF16)


def rate(hamilton, state):
    sign = jnp.where(low_half(state.shape), 1.0, -1.0).astype(F32)
    turned_s = pltpu.roll(state, NB, 1) * sign
    turned_h = pltpu.roll(hamilton, NB, 1) * sign
    right_high, right_low = halves(
        jnp.concatenate([turned_s, state, turned_h, hamilton], axis=0)
    )
    left_high, left_low = halves(jnp.concatenate([hamilton, -state], axis=1))
    left = jnp.concatenate([left_high, left_low], axis=0)
    right = jnp.concatenate([right_high, right_low], axis=1)
    out = jnp.dot(left, right, preferred_element_type=F32)
    return out[:NB, :TILE] + (out[:NB, TILE:] + out[NB:, :TILE])


def kernel(
    dens_hbm, h_hbm, coup_hbm, donors_hbm, counts_hbm, out,
    dens, hraw, coup, donors, counts, low0, halo0, mix, hband, state, ham, change, sigma,
    whole_s, whole_r, enc_s, enc_r, scale_s, scale_r, mid_s, mid_r, halo1,
    load_sem, enc_ss, enc_rs, scale_ss, scale_rs, last_rs, last_scale_rs,
    mid_ss, mid_rs, halo0_ss, halo0_rs, halo1_ss, halo1_rs,
):
    me = lax.axis_index("ba")
    mine = lax.axis_index("ka")
    ring = lax.axis_size("ka")
    sides = (lax.rem(mine + 1, ring), lax.rem(mine + ring - 1, ring))

    pairs = (
        (dens_hbm, dens),
        (coup_hbm, coup),
        (h_hbm, hraw),
        (donors_hbm, donors),
        (counts_hbm, counts),
    )
    loads = [pltpu.make_async_copy(a, b, load_sem.at[i]) for i, (a, b) in enumerate(pairs)]
    loads[0].start()

    barrier = pltpu.get_barrier_semaphore()
    for i in range(1, GROUP):
        pl.semaphore_signal(
            barrier, inc=1, device_id={"ba": lax.rem(me + i, GROUP)}, device_id_type=MESH
        )
    for side in sides:
        pl.semaphore_signal(barrier, inc=1, device_id={"ka": side}, device_id_type=MESH)

    def partner(i):
        step = (1 - 2 * lax.rem(i, 2)) * ((i + 1) // 2)
        return lax.rem(me + GROUP // 2 + step, GROUP)

    def to_ba(src, dst, send_sem, recv_sem, there):
        return pltpu.make_async_remote_copy(
            src_ref=src,
            dst_ref=dst,
            send_sem=send_sem,
            recv_sem=recv_sem,
            device_id={"ba": there},
            device_id_type=MESH,
        )

    def to_ka(src, dst, send_sem, recv_sem, side):
        return pltpu.make_async_remote_copy(
            src_ref=src,
            dst_ref=dst,
            send_sem=send_sem,
            recv_sem=recv_sem,
            device_id={"ka": sides[side]},
            device_id_type=MESH,
        )

    others = pl.ds(0, GROUP - 1)

    def codes_of(slot, sending, which):
        if slot == 0:
            return (whole_s if sending else whole_r).at[which]
        ref = enc_s if sending else enc_r
        if slot < 6:
            return ref.at[slot - 1, which]
        return ref.at[5, which, pl.ds((slot - 6) * QUAD_ROWS, QUAD_ROWS)]

    def enc_copy(slot, there, group):
        return to_ba(
            codes_of(slot, True, there),
            codes_of(slot, False, me),
            enc_ss.at[slot],
            enc_rs.at[slot] if slot < 7 else last_rs.at[group],
            there,
        )

    def enc_all(slot, which=others, group=0):
        ref = codes_of(slot, False, which)
        recv_sem = enc_rs.at[slot] if slot < 7 else last_rs.at[group]
        return to_ba(ref, ref, enc_ss.at[slot], recv_sem, me)

    def scale_copy(slot, there, group):
        return to_ba(
            scale_s.at[slot, there],
            scale_r.at[slot, me],
            scale_ss.at[slot],
            scale_rs.at[slot] if slot < 7 else last_scale_rs.at[group],
            there,
        )

    def scale_all(slot, which=others, group=0):
        ref = scale_r.at[slot, which]
        recv_sem = scale_rs.at[slot] if slot < 7 else last_scale_rs.at[group]
        return to_ba(ref, ref, scale_ss.at[slot], recv_sem, me)

    def halo0_copy(side, chunk):
        cut = pl.ds(2 * chunk, 2)
        return to_ka(
            low0.at[cut],
            halo0.at[side, cut],
            halo0_ss.at[side, chunk],
            halo0_rs.at[side, chunk],
            side,
        )

    def mid_copy(half, there, group):
        cut = pl.ds(half * PART, PART)
        return to_ba(
            mid_s.at[there, :, cut],
            mid_r.at[me, :, cut],
            mid_ss.at[half],
            mid_rs.at[half, group],
            there,
        )

    def mid_group(half, which, group):
        ref = mid_r.at[which, :, pl.ds(half * PART, PART)]
        return to_ba(ref, ref, mid_ss.at[half], mid_rs.at[half, group], me)

    def halo1_copy(side, half, src):
        cut = pl.ds(half * PART, PART)
        return to_ka(
            mid_r.at[src, :, cut],
            halo1.at[side, src, :, cut],
            halo1_ss.at[side],
            halo1_rs.at[side],
            side,
        )

    def halo1_all(side):
        return to_ka(mid_r, halo1.at[side], halo1_ss.at[side], halo1_rs.at[side], side)

    def momenta(block, half):
        return pl.ds(pl.multiple_of(block * GROUP + half * PART, PART), PART)

    def rows(half, block):
        return pl.ds(pl.multiple_of(half * HALF + block * ROWS, ROWS), ROWS)

    def parts_of(there):
        return [sigma[:, momenta(there, half), :].reshape(ROWS, TILE) for half in range(2)]

    def by_partner(put, start, near=False):
        def body(n, carry):
            order = [GROUP - 2 - 3 * n - i if near else 3 * n + i for i in range(3)]
            for i in order:
                put(i, partner(i))
            for i in order:
                start(i, partner(i))
            return carry

        lax.fori_loop(0, (GROUP - 1) // 3, body, 0)

    def send_codes(slot, put):
        def start(i, there):
            enc_copy(slot, there, (i + 1) // 2).start()
            scale_copy(slot, there, (i + 1) // 2).start()

        sending = whole_s if slot == 0 else enc_s
        by_partner(lambda i, there: put(sending, scale_s, there, there), start)
        put(whole_r if slot == 0 else enc_r, scale_r, me, me)

    loads[0].wait()
    for load in loads[1:]:
        load.start()
    for t in range(2):
        cut = pl.ds(t * TILE, TILE)
        for a, values in zip((2 * t, 2 * t + 1), merge(dens[0, :, cut], dens[1, :, cut])):
            low0[a] = values.astype(BF16)
            sigma[a] = values
        if t == 0:
            pl.semaphore_wait(barrier, GROUP + 1)
        for side in range(2):
            halo0_copy(side, t).start()

    def put_whole(codes_ref, scale_ref, slot, there):
        codes, scale = encode(*parts_of(there))
        for half in range(2):
            codes_ref[slot, pl.ds(half * ROWS, ROWS), :] = codes[half]
        scale_ref[0, slot] = scale

    send_codes(0, put_whole)

    for load in (loads[1], loads[3], loads[4]):
        load.wait()
    for t in range(2):
        tile = mine * 2 + t
        for position in range(2 + 2 * REACH):
            block = jnp.zeros((TILE, TILE), F32)
            if 0 <= position - t <= 2 * REACH:
                for s in range(ND):
                    offset = lax.rem(donors[t, s] - tile + REACH + TILES, TILES)
                    used = jnp.logical_and(offset == position - t, counts[t] > s)
                    weight = jnp.where(used, -1.0, 0.0).astype(F32)
                    block = block + coup[t, s].astype(F32) * weight
            mix[pl.ds(t * TILE, TILE), pl.ds(position * TILE, TILE)] = block.astype(BF16)

    def mixed(block, values):
        cut = pl.ds(block * 2 * TILE, 2 * TILE)
        return jnp.dot(mix[:, cut], values, preferred_element_type=F32)

    for a in range(4):
        sigma[a] = mixed(1, low0[a])

    loads[2].wait()

    def lay(step, carry):
        for i in range(4):
            t = step * 4 + i
            cut = pl.ds(pl.multiple_of(t * TILE, TILE), TILE)
            for half in range(2):
                part = pl.ds(half * PART, PART)
                first, second = merge(hraw[0, part, cut], hraw[1, part, cut])
                base = pl.multiple_of(half * HALF + t * 2 * PART, 2 * PART)
                hband[pl.ds(base, PART), :] = first
                hband[pl.ds(base + PART, PART), :] = second
        return carry

    lax.fori_loop(0, NB // 8, lay, 0)

    for chunk in range(2):
        for side in range(2):
            halo0_copy(side, chunk).wait_recv()
        bands = pl.ds(2 * chunk, 2)
        for a in (2 * chunk, 2 * chunk + 1):
            sigma[a] += mixed(0, halo0[0, a]) + mixed(2, halo0[1, a])

        def put_bands(codes_ref, scale_ref, slot, there, chunk=chunk, bands=bands):
            parts = [
                sigma[bands, momenta(there, half), :].reshape(ROWS // 2, TILE) for half in range(2)
            ]
            codes, scale = encode(*parts)
            for half in range(2):
                codes_ref[chunk, slot, pl.ds(half * ROWS // 2, ROWS // 2), :] = codes[half]
            scale_ref[1 + chunk, slot] = scale

        send_codes(1 + chunk, put_bands)

    scale_all(0).wait_recv()
    enc_all(0).wait_recv()

    def take_state(src, carry):
        values = decode(whole_r[src], scale_r[0, src])
        for half in range(2):
            state[rows(half, src), :] = values[half * ROWS : (half + 1) * ROWS]
        return carry

    lax.fori_loop(0, GROUP, take_state, 0)

    for chunk in range(2):
        scale_all(1 + chunk).wait_recv()
        enc_all(1 + chunk).wait_recv()

        def take_bands(src, carry, chunk=chunk):
            values = decode(enc_r[chunk, src], scale_r[1 + chunk, src])
            for half in range(2):
                base = half * HALF + src * ROWS + chunk * ROWS // 2
                cut = pl.ds(pl.multiple_of(base, ROWS // 2), ROWS // 2)
                ham[cut, :] = hband[cut, :] + values[half * ROWS // 2 : (half + 1) * ROWS // 2]
            return carry

        lax.fori_loop(0, GROUP, take_bands, 0)

    def each_momentum(half, use, quads=(0, 1)):
        def step(quad, carry):
            cuts = [pl.ds(half * HALF + quad * QUAD + i, NB, stride=PART) for i in range(QUAD)]
            states = [state[cut, :] for cut in cuts]
            rates = [rate(ham[cut, :], here) for cut, here in zip(cuts, states)]
            for i in range(QUAD):
                use(quad, i, cuts[i], states[i], rates[i])
            return carry

        lax.fori_loop(quads[0], quads[-1] + 1, step, 0)

    def to_middle(quad, i, cut, here, gained):
        state[cut, :] = here + (0.5 * step_size) * gained

    def to_change(quad, i, cut, here, gained):
        change[cut, :] = step_size * gained

    def to_last(quad, i, cut, here, gained):
        change[pl.ds(HALF + quad * NB * QUAD + i, NB, stride=QUAD), :] = step_size * gained

    for half in range(2):
        each_momentum(half, to_middle)
        part = pl.ds(half * PART, PART)

        def put_mid(i, there, half=half, part=part):
            values = state[rows(half, there), :].astype(BF16)
            mid_s[there, :, part, :] = values.reshape(4, PART, TILE)

        def start_mid(i, there, half=half):
            mid_copy(half, there, (i + 1) // 2).start()

        by_partner(put_mid, start_mid, near=True)
        mid_r[me, :, part, :] = state[rows(half, me), :].astype(BF16).reshape(4, PART, TILE)

    for half in range(2):
        for side in range(2):
            halo1_copy(side, half, me).start()

    def forward(half, group):
        members = [2 * group, 2 * group - 1] if group > 0 else [0]
        mid_group(half, pl.ds(0, len(members)), group).wait_recv()
        for i in members:
            for side in range(2):
                halo1_copy(side, half, partner(i)).start()

    for group in (7, 6, 5):
        forward(0, group)
    for group in (4, 3, 2, 1, 0):
        forward(0, group)
        forward(1, group + 3)
    for group in (2, 1, 0):
        forward(1, group)

    def band(ref, a):
        return ref[:, a].reshape(2 * TILE, TILE)

    for a in range(4):
        sigma[a] = mixed(1, band(mid_r, a))
    for side in range(2):
        halo1_all(side).wait_recv()
    for a in range(4):
        sigma[a] += mixed(0, band(halo1.at[0], a)) + mixed(2, band(halo1.at[1], a))

    for half in range(2):

        def put_momenta(codes_ref, scale_ref, slot, there, half=half):
            (codes,), scale = encode(parts_of(there)[half])
            codes_ref[2 + half, slot] = codes
            scale_ref[3 + half, slot] = scale

        send_codes(3 + half, put_momenta)

    for half in range(2):
        scale_all(3 + half).wait_recv()
        enc_all(3 + half).wait_recv()

        def take_momenta(src, carry, half=half):
            cut = rows(half, src)
            ham[cut, :] = hband[cut, :] + decode(enc_r[2 + half, src], scale_r[3 + half, src])
            return carry

        lax.fori_loop(0, GROUP, take_momenta, 0)
        if half == 0:
            each_momentum(0, to_change)

            def put_change(codes_ref, scale_ref, index, there):
                (codes,), scale = encode(change[rows(0, there), :])
                codes_ref[4, index] = codes
                scale_ref[5, index] = scale

            send_codes(5, put_change)

    for quad in range(2):
        each_momentum(1, to_last, (quad,))

        def put_last(codes_ref, scale_ref, index, there, quad=quad):
            base = HALF + quad * NB * QUAD + there * QUAD_ROWS
            (codes,), scale = encode(change[pl.ds(pl.multiple_of(base, QUAD_ROWS), QUAD_ROWS), :])
            codes_ref[5, index, pl.ds(quad * QUAD_ROWS, QUAD_ROWS), :] = codes
            scale_ref[6 + quad, index] = scale

        send_codes(6 + quad, put_last)

    for side in range(2):
        halo1_all(side).wait_send()
        for chunk in range(2):
            halo0_copy(side, chunk).wait_send()
    for half in range(2):
        ref = mid_s.at[others, :, pl.ds(half * PART, PART)]
        to_ba(ref, ref, mid_ss.at[half], mid_rs.at[half, 0], me).wait_send()
    for slot in range(5):
        enc_all(slot).wait_send()
        scale_all(slot).wait_send()

    def finish(half, sources):
        done = []
        for src in sources:
            part = momenta(src, half)
            if half == 0:
                gained = decode(enc_r[4, src], scale_r[5, src])
                bands = [gained[a * PART : (a + 1) * PART] for a in range(4)]
            else:
                quads = [
                    decode(
                        enc_r[5, src, pl.ds(quad * QUAD_ROWS, QUAD_ROWS), :], scale_r[6 + quad, src]
                    )
                    for quad in range(2)
                ]
                bands = [
                    jnp.concatenate([values[a * QUAD : (a + 1) * QUAD] for values in quads], axis=0)
                    for a in range(4)
                ]
            for t in range(2):
                cut = pl.ds(t * TILE, TILE)
                for c, change_c in enumerate(split(bands[2 * t], bands[2 * t + 1])):
                    done.append((c, part, cut, dens[c, part, cut] + change_c))
        for c, part, cut, values in done:
            out[c, part, cut] = values

    scale_all(5).wait_recv()
    enc_all(5).wait_recv()

    def finish_first(step, carry):
        finish(0, [step * 4 + i for i in range(4)])
        return carry

    lax.fori_loop(0, GROUP // 4, finish_first, 0)
    scale_all(6).wait_recv()
    enc_all(6).wait_recv()
    finish(1, [me])

    def finish_group(group, members):
        which = pl.ds(0, len(members))
        enc_all(7, which, group).wait_recv()
        scale_all(7, which, group).wait_recv()
        finish(1, [partner(i) for i in members])

    finish_group(0, [0])

    def finish_pair(group, carry):
        finish_group(group, [2 * group - 1, 2 * group])
        return carry

    lax.fori_loop(1, GROUP // 2, finish_pair, 0)
    for slot in (5, 6, 7):
        enc_all(slot).wait_send()
        scale_all(slot).wait_send()


def local(density, h_bands, coupling, donors, counts):
    whole = (GROUP, 2 * ROWS, TILE)
    codes = (6, GROUP, ROWS, TILE)
    scales = (8, GROUP, 1, TILE)
    middle = (GROUP, 4, GROUP, TILE)
    big = (NB * GROUP, TILE)
    dma = pltpu.SemaphoreType.DMA
    anywhere = pl.BlockSpec(memory_space=pl.ANY)
    operands = [
        pltpu.with_memory_space_constraint(x, pltpu.HBM)
        for x in (density, h_bands, coupling, donors, counts)
    ]
    return pl.pallas_call(
        kernel,
        out_shape=pltpu.VMEM(density.shape, F32),
        in_specs=[anywhere] * 5,
        out_specs=pl.BlockSpec(memory_space=pltpu.VMEM),
        scratch_shapes=[
            pltpu.VMEM(density.shape, F32),
            pltpu.VMEM(h_bands.shape, F32),
            pltpu.VMEM(coupling.shape, BF16),
            pltpu.SMEM(donors.shape, jnp.int32),
            pltpu.SMEM(counts.shape, jnp.int32),
            pltpu.VMEM((4, 2 * TILE, TILE), BF16),
            pltpu.VMEM((2, 4, 2 * TILE, TILE), BF16),
            pltpu.VMEM((2 * TILE, 6 * TILE), BF16),
            pltpu.VMEM(big, F32),
            pltpu.VMEM(big, F32),
            pltpu.VMEM(big, F32),
            pltpu.VMEM(big, F32),
            pltpu.VMEM((4, 2 * TILE, TILE), F32),
            pltpu.VMEM(whole, I16),
            pltpu.VMEM(whole, I16),
            pltpu.VMEM(codes, I16),
            pltpu.VMEM(codes, I16),
            pltpu.VMEM(scales, F32),
            pltpu.VMEM(scales, F32),
            pltpu.VMEM(middle, BF16),
            pltpu.VMEM(middle, BF16),
            pltpu.VMEM((2, *middle), BF16),
            dma((5,)),
            dma((8,)),
            dma((7,)),
            dma((8,)),
            dma((7,)),
            dma((GROUP // 2,)),
            dma((GROUP // 2,)),
            dma((2,)),
            dma((2, GROUP // 2)),
            dma((2, 2)),
            dma((2, 2)),
            dma((2,)),
            dma((2,)),
        ],
        compiler_params=pltpu.CompilerParams(
            collective_id=0, has_side_effects=True, vmem_limit_bytes=40 << 20
        ),
    )(*operands)


def solution(mesh):
    placed = (
        P(None, "ka", "ba"),
        P(None, ("ka", "ba"), None),
        P("ka", None, None, None),
        P("ka", None),
        P("ka"),
    )
    return jax.shard_map(
        local, mesh=mesh, in_specs=placed, out_specs=P(None, "ka", "ba"), check_vma=False
    )
```
